32 devices in a mesh: sec: 8 (over z, core), term: 4 (over y, x).
Axes of the slice: x: 2, y: 2, z: 4, core: 2. Of those that a mesh axis runs over, the one named last changes fastest.
Arguments:
- psi: bfloat16 [8, 512, 512], P('sec'), may hold values from -6 to 6
- left_ops: bfloat16 [8, 24, 512, 512], P('sec', 'term'), may hold values from -0.078125 to 0.078125
- right_ops: bfloat16 [8, 24, 512, 512], P('sec', 'term'), may hold values from -0.078125 to 0.078125
- term_mask: int32 [8, 24], P('sec', 'term'), may hold values 0 or 1
- pair_src: int32 [8], P('sec'), may hold values from 0 to 7, each once
- pair_dst: int32 [8], P('sec'), may hold values from 0 to 7, each once
Outputs:
- sigma: bfloat16 [8, 512, 512], P('sec')
The draws below stay inside these ranges and needn't reach their ends.
Inputs may be any that keep to these rules, and one draw needn't show every extreme that they name: `pair_src`: each of the 8 sector blocks is the source of exactly one pair. `pair_dst`: each of the 8 sector blocks is the target of exactly one pair.
All inputs are finite; a program needn't handle non-finite values. No bound on the sum of `term_mask` on one device may be relied on, other than what follows from the above.
Results may differ from the reference program's by a relative error of at most 0.0065.
Values may be sent and summed in bfloat16 or wider, within the bound.
No kernel may reach another device: no remote copies, remote signals or barrier semaphores. Data moves between devices by JAX's collectives and lax.ppermute only.
A program may use at most 64 MiB of HBM per device.

```python
import jax
import jax.numpy as jnp
from jax import lax

BLK = 512
NSEC = 8
TERMS = 24


def place_ends(drawn, own_key, low, top_value):
    longest = drawn.shape.index(max(drawn.shape))
    spots = []
    for shift in (0, 1):
        where = [jax.random.randint(jax.random.fold_in(own_key, axis), (), 0, length) for axis, length in enumerate(drawn.shape)]
        where[longest] = (where[longest] + shift) % drawn.shape[longest]
        spots.append(tuple(where))
    return drawn.at[spots[0]].set(low).at[spots[1]].set(top_value)


def levels(key, shape, shards, smallest, high):
    factor_of, own = 1.0, jax.random.fold_in(key, 6)
    for position, parts in shards:
        heights = jnp.exp(jax.random.uniform(jax.random.fold_in(own, position), (parts,), jnp.float32, smallest / len(shards), high / len(shards)))
        factor_of = factor_of * jnp.repeat(heights, shape[position] // parts).reshape([-1 if axis == position else 1 for axis in range(len(shape))])
    return factor_of


def centred(stream_key, extent, spread, reach, shards=(), held_as=jnp.bfloat16):
    result = spread * jax.random.normal(stream_key, extent, jnp.float32)
    if shards:
        result = result * levels(stream_key, extent, shards, -0.22, 0.18)
    return jnp.clip(result, -reach, reach).astype(held_as)


def setup_inputs(seed: int = 0) -> dict:
    streams_of = jax.random.split(jax.random.key(seed), 7)
    psi = centred(streams_of[0], (NSEC, BLK, BLK), 1.0, 6.0, ((0, 8),))
    left_ops = centred(streams_of[1], (NSEC, TERMS, BLK, BLK), (BLK * 12) ** -0.5, 0.078125, ((0, 8), (1, 4)))
    right_ops = centred(streams_of[2], (NSEC, TERMS, BLK, BLK), (BLK * 12) ** -0.5, 0.078125, ((0, 8), (1, 4)))
    term_mask = place_ends((jax.random.randint(streams_of[3], (NSEC, TERMS), 0, 2) < 1).astype(jnp.int32), jax.random.fold_in(streams_of[3], 1), 0, 1)
    pair_src = jax.random.permutation(streams_of[4], NSEC).astype(jnp.int32)
    pair_dst = jax.random.permutation(streams_of[5], NSEC).astype(jnp.int32)
    return {"psi": psi, "left_ops": left_ops, "right_ops": right_ops, "term_mask": term_mask, "pair_src": pair_src, "pair_dst": pair_dst}


def reference(psi, left_ops, right_ops, term_mask, pair_src, pair_dst):
    zero_block = jnp.zeros((BLK, BLK), jnp.float32)

    def pair_step(sigma_acc, index):
        source = pair_src[index]
        target = pair_dst[index]
        src_block = psi[source]
        dst_block = psi[target]

        def term_step(acc, term):
            def active(carry):
                fwd_acc, adj_acc = carry
                left = left_ops[index, term]
                right = right_ops[index, term]
                inner_fwd = jnp.dot(left, src_block, preferred_element_type=jnp.float32).astype(jnp.bfloat16)
                inner_adj = jnp.dot(left.T, dst_block, preferred_element_type=jnp.float32).astype(jnp.bfloat16)
                fwd_acc = fwd_acc + jnp.dot(inner_fwd, right.T, preferred_element_type=jnp.float32)
                adj_acc = adj_acc + jnp.dot(inner_adj, right, preferred_element_type=jnp.float32)
                return fwd_acc, adj_acc

            return lax.cond(term_mask[index, term] == 1, active, lambda carry: carry, acc), None

        (fwd, adj), _ = lax.scan(term_step, (zero_block, zero_block), jnp.arange(TERMS, dtype=jnp.int32))
        sigma_acc = sigma_acc.at[target].add(fwd)
        sigma_acc = sigma_acc.at[source].add(adj)
        return sigma_acc, None

    start = jnp.zeros((NSEC, BLK, BLK), jnp.float32)
    total, _ = lax.scan(pair_step, start, jnp.arange(NSEC, dtype=jnp.int32))
    return total.astype(jnp.bfloat16)
```

```python
import functools

import jax
import jax.numpy as jnp
from jax import lax
from jax.experimental import pallas as pl
from jax.experimental.pallas import tpu as pltpu
from jax.sharding import PartitionSpec as P


F32 = jnp.float32
BF16 = jnp.bfloat16


def shifted(own, step, count):
    if count & (count - 1) == 0:
        return own ^ step
    return lax.rem(own + step, count) if not isinstance(own, int) else (own + step) % count


def back(own, step, count):
    if count & (count - 1) == 0:
        return own ^ step
    return lax.rem(own + count - step, count)


def side_kernel(terms, groups, adjoint, t_ref, mask_ref, *refs):
    pieces, left, right = refs[:groups], refs[groups], refs[groups + 1]
    outs = refs[groups + 2 : 2 * groups + 2]
    psi, lbuf, rbuf, acc, lsem, rsem = refs[2 * groups + 2 :]
    rows = pieces[0].shape[0]
    t = t_ref[0]

    def copies(i):
        return (
            pltpu.make_async_copy(left.at[0, i], lbuf.at[i], lsem.at[i]),
            pltpu.make_async_copy(right.at[0, i], rbuf.at[i], rsem.at[i]),
        )

    for i in range(terms):

        @pl.when(mask_ref[0, i] == 1)
        def _():
            for copy in copies(i):
                copy.start()

    for d in range(groups):
        at = pl.multiple_of(back(t, d, groups) * rows, rows)
        psi[pl.ds(at, rows), :] = pieces[d][...]
    acc[...] = jnp.zeros_like(acc)

    def step(i, carry):
        @pl.when(mask_ref[0, i] == 1)
        def _():
            cl, cr = copies(i)
            cl.wait()
            if adjoint:
                inner = lax.dot_general(
                    lbuf[i], psi[...], (((0,), (0,)), ((), ())), preferred_element_type=F32
                ).astype(BF16)
            else:
                inner = jnp.dot(lbuf[i], psi[...], preferred_element_type=F32).astype(BF16)
            cr.wait()
            acc[...] += lax.dot_general(
                inner,
                rbuf[i],
                (((1,), (0 if adjoint else 1,)), ((), ())),
                preferred_element_type=F32,
            )

        return carry

    lax.fori_loop(0, terms, step, 0)
    for d in range(groups):
        at = pl.multiple_of(shifted(t, d, groups) * rows, rows)
        outs[d][...] = acc[pl.ds(at, rows), :].astype(BF16)


def side(adjoint, t, mask, pieces, left, right):
    groups, terms, order = len(pieces), left.shape[1], left.shape[2]
    rows = pieces[0].shape[0]
    vmem, smem = pl.BlockSpec(memory_space=pltpu.VMEM), pl.BlockSpec(memory_space=pltpu.SMEM)
    hbm = pl.BlockSpec(memory_space=pl.ANY)
    return pl.pallas_call(
        functools.partial(side_kernel, terms, groups, adjoint),
        out_shape=[jax.ShapeDtypeStruct((rows, order), BF16)] * groups,
        in_specs=[smem, smem] + [vmem] * groups + [hbm, hbm],
        out_specs=[vmem] * groups,
        scratch_shapes=[
            pltpu.VMEM((order, order), BF16),
            pltpu.VMEM((terms, order, order), BF16),
            pltpu.VMEM((terms, order, order), BF16),
            pltpu.VMEM((order, order), F32),
            pltpu.SemaphoreType.DMA((terms,)),
            pltpu.SemaphoreType.DMA((terms,)),
        ],
        name="adj_side" if adjoint else "fwd_side",
        cost_estimate=pl.CostEstimate(
            flops=4 * terms * order**3, bytes_accessed=4 * terms * order**2, transcendentals=0
        ),
    )(t, mask, *pieces, left, right)


def local(nsec, nterm, psi, left_ops, right_ops, term_mask, pair_src, pair_dst):
    order = psi.shape[1]
    rows = order // nterm
    half = rows // 2
    chips = nsec // 2
    k = lax.axis_index("sec").astype(jnp.int32)
    t = lax.axis_index("term").astype(jnp.int32)
    z, core = k // 2, k % 2
    swap = [(i, i ^ 1) for i in range(nsec)]

    def zrot(d):
        return [(i, (i + 2 * d) % nsec) for i in range(nsec)]

    def tperm(d):
        return [(i, shifted(i, d, nterm)) for i in range(nterm)]

    src, dst = pair_src[0], pair_dst[0]
    other = lax.ppermute(jnp.concatenate([pair_src, pair_dst]), "sec", swap)
    src_o, dst_o = other[0], other[1]

    own = lax.dynamic_slice(psi[0], (t * rows, 0), (rows, order))
    mine = [own] + [lax.ppermute(own, "sec", zrot(d)) for d in range(1, chips)]
    theirs = [lax.ppermute(b, "sec", swap) for b in mine]
    names = [lax.rem(z + chips - d, chips) * 2 + core for d in range(chips)]

    def pick(label):
        out = jnp.zeros((rows, order), BF16)
        for b, o, n in zip(mine, theirs, names):
            out = jnp.where(label == n, b, out)
            out = jnp.where(label == (n ^ 1), o, out)
        return out

    def spread(x):
        return [x] + [lax.ppermute(x, "term", tperm(d)) for d in range(1, nterm)]

    src_pieces = spread(pick(src))
    dst_pieces = spread(pick(dst))
    tt = t[None]
    fwd = side(False, tt, term_mask, src_pieces, left_ops, right_ops)
    adj = side(True, tt, term_mask, dst_pieces, left_ops, right_ops)

    def gather_sum(parts):
        total = parts[0].astype(F32)
        for d in range(1, nterm):
            total = total + lax.ppermute(parts[d], "term", tperm(d)).astype(F32)
        return total

    f, a = gather_sum(fwd), gather_sum(adj)
    both = jnp.stack([f, a]).astype(BF16)
    low, high = both[:, :half], both[:, half:]
    keep = jnp.where(core == 0, low, high)
    got = lax.ppermute(jnp.where(core == 0, high, low), "sec", swap)

    def slot(s):
        zero = jnp.zeros((half, order), F32)
        return (
            jnp.where(dst == s, keep[0].astype(F32), zero)
            + jnp.where(src == s, keep[1].astype(F32), zero)
            + jnp.where(dst_o == s, got[0].astype(F32), zero)
            + jnp.where(src_o == s, got[1].astype(F32), zero)
        )

    total = None
    for d in range(chips):
        to = lax.rem(z + d, chips)
        part = jnp.stack([slot(2 * to), slot(2 * to + 1)])
        if d:
            part = lax.ppermute(part.astype(BF16), "sec", zrot(d)).astype(F32)
        total = part if total is None else total + part
    total = total.astype(BF16)
    stay = jnp.where(core == 0, total[0], total[1])
    come = lax.ppermute(jnp.where(core == 0, total[1], total[0]), "sec", swap)
    piece = jnp.concatenate(
        [jnp.where(core == 0, stay, come), jnp.where(core == 0, come, stay)], axis=0
    )
    out = jnp.zeros((order, order), BF16)
    for d, p in enumerate(spread(piece)):
        out = lax.dynamic_update_slice(out, p, (back(t, d, nterm) * rows, 0))
    return out[None]


def solution(mesh):
    placed = (
        P("sec", None, None),
        P("sec", "term", None, None),
        P("sec", "term", None, None),
        P("sec", "term"),
        P("sec"),
        P("sec"),
    )
    return jax.shard_map(
        functools.partial(local, mesh.shape["sec"], mesh.shape["term"]),
        mesh=mesh,
        in_specs=placed,
        out_specs=P("sec", None, None),
        check_vma=False,
    )
```
